256 devices in a mesh: node: 32 (over x_hi, z, core), feat: 8 (over x_lo, y).
Axes of the slice: x: 4 (x_hi: 2, x_lo: 2; x = x_hi * 2 + x_lo), y: 4, z: 8, core: 2. Of those that a mesh axis runs over, the one named last changes fastest.
Arguments:
- features: bfloat16 [512, 131072], P('feat', 'node'), may hold values from -6 to 6
- tiles: bfloat16 [7680, 128, 128], P('node')
- tile_rows: int32 [7680], P('node'), may hold values from 0 to 31
- tile_cols: int32 [7680], P('node'), may hold values from 0 to 31
- counts: int32 [160], P('node'), may hold values from 12 to 48, as said below
- weight_one: bfloat16 [512, 512], replicated, may hold values from -0.25 to 0.25
- weight_two: bfloat16 [512, 512], replicated, may hold values from -0.25 to 0.25
- cotangent: bfloat16 [512, 131072], P('feat', 'node'), may hold values from -6 to 6
Outputs:
- layer_out: bfloat16 [512, 131072], P('feat', 'node')
- feature_grad: bfloat16 [512, 131072], P('feat', 'node')
- weight_one_grad: float32 [512, 512], P('feat')
- weight_two_grad: float32 [512, 512], P('feat')
The draws below stay inside these ranges and needn't reach their ends.
Inputs may be any that keep to these rules, and one draw needn't show every extreme that they name: Slots at or beyond counts[p * 5 + o] are not part of A. Some entry equals 48 in every draw.
All inputs are finite; a program needn't handle non-finite values.
Results may differ from the reference program's by a relative error of at most 0.0051.
Values may be sent and summed in bfloat16 or wider, within the bound.
A program may use at most 128 MiB of HBM per device.

```python
import jax
import jax.numpy as jnp
from jax import lax

H = 512
BLOCK = 128
REACH = 2
RB = 32
SLOTS = 48
OFFS = 5
NODES = 131072
TILES = 7680
COUNTS = 160
N_NODE = 32


def draw_tiles(key, part):
    key_mask = jax.random.fold_in(key, 11)
    key_value = jax.random.fold_in(key, 12)
    present = jax.random.randint(key_mask, (TILES, BLOCK, BLOCK), 0, 2).astype(jnp.float32)
    values = jax.random.uniform(key_value, (TILES, BLOCK, BLOCK), jnp.float32, 0.2, 1.0)
    expected = OFFS * SLOTS * 0.6 * 0.5 * BLOCK / RB
    factor = 1.0 / max(expected, 1.0) ** 0.5
    return (present * values * factor).astype(jnp.bfloat16)


def draw_counts(key, part):
    key_count = jax.random.fold_in(key, 21)
    key_place = jax.random.fold_in(key, 22)
    drawn = jax.random.randint(key_count, (COUNTS,), max(1, SLOTS // 4), SLOTS + 1)
    place = jax.random.randint(key_place, (), 0, COUNTS)
    return jnp.where(jnp.arange(COUNTS, dtype=jnp.int32) == place, SLOTS, drawn).astype(jnp.int32)


def touch_ends(result, key, low, largest):
    longest = result.shape.index(max(result.shape))
    spots = []
    for shift in (0, 1):
        where = [jax.random.randint(jax.random.fold_in(key, axis), (), 0, length) for axis, length in enumerate(result.shape)]
        where[longest] = (where[longest] + shift) % result.shape[longest]
        spots.append(tuple(where))
    return result.at[spots[0]].set(low).at[spots[1]].set(largest)


def steps_of(stream_key, dims, shards, low, top_value):
    loudness, own = 1.0, jax.random.fold_in(stream_key, 6)
    for position, shards_of in shards:
        heights = jnp.exp(jax.random.uniform(jax.random.fold_in(own, position), (shards_of,), jnp.float32, low / len(shards), top_value / len(shards)))
        loudness = loudness * jnp.repeat(heights, dims[position] // shards_of).reshape([-1 if axis == position else 1 for axis in range(len(dims))])
    return loudness


def scatter_about(own_key, dims, deviation, bound, shards=(), kind=jnp.bfloat16):
    values = jax.random.normal(own_key, dims, jnp.float32) * deviation
    if len(shards) > 0:
        values = steps_of(own_key, dims, shards, -0.22, 0.18) * values
    return jnp.clip(values, min=-bound, max=bound).astype(kind)


def setup_inputs(seed: int = 0) -> dict:
    arg_keys = jax.random.split(jax.random.key(seed), 9)
    return {
        "features": scatter_about(arg_keys[0], (H, NODES), 1.0, 6.0, ((0, 8), (1, 32))),
        "tiles": draw_tiles(jax.random.fold_in(arg_keys[8], 71), 0),
        "tile_rows": touch_ends(jax.random.randint(arg_keys[2], (TILES,), 0, RB), jax.random.fold_in(arg_keys[2], 1), 0, RB - 1).astype(jnp.int32),
        "tile_cols": touch_ends(jax.random.randint(arg_keys[3], (TILES,), 0, RB), jax.random.fold_in(arg_keys[3], 1), 0, RB - 1).astype(jnp.int32),
        "counts": draw_counts(jax.random.fold_in(arg_keys[8], 71), 0),
        "weight_one": scatter_about(arg_keys[5], (H, H), H ** -0.5, 0.25),
        "weight_two": scatter_about(arg_keys[6], (H, H), H ** -0.5, 0.25),
        "cotangent": scatter_about(arg_keys[7], (H, NODES), 1.0, 6.0, ((0, 8), (1, 32))),
    }


def tile_tables(tiles, tile_rows, tile_cols, counts):
    tile_set = tiles.reshape(N_NODE, OFFS, SLOTS, BLOCK, BLOCK)
    slot_rows = tile_rows.reshape(N_NODE, OFFS, SLOTS)
    slot_cols = tile_cols.reshape(N_NODE, OFFS, SLOTS)
    live = jnp.arange(SLOTS, dtype=jnp.int32)[None, None, :] < counts.reshape(N_NODE, OFFS)[:, :, None]
    return tile_set, slot_rows, slot_cols, live


def aggregate(field, tables):
    tile_set, slot_rows, slot_cols, live = tables
    width = field.shape[0]
    panels = field.reshape(width, N_NODE, RB, BLOCK)
    block_ids = jnp.arange(RB, dtype=jnp.int32)

    def target(part):
        total = jnp.zeros((width, RB, BLOCK), jnp.float32)
        for offset in range(OFFS):
            source = (part + offset - REACH) % N_NODE
            panel = jnp.take(panels, source, axis=1)
            pieces = jnp.take(panel, slot_cols[part, offset], axis=1)
            partial_out = jnp.einsum('hsk,srk->hsr', pieces.astype(jnp.float32), tile_set[part, offset].astype(jnp.float32), precision=lax.Precision.HIGHEST)
            selector = ((slot_rows[part, offset][None, :] == block_ids[:, None]) & live[part, offset][None, :]).astype(jnp.float32)
            total = total + jnp.einsum('hsr,bs->hbr', partial_out, selector, precision=lax.Precision.HIGHEST)
        return total

    stacked = lax.map(target, jnp.arange(N_NODE, dtype=jnp.int32))
    return jnp.transpose(stacked, (1, 0, 2, 3)).reshape(width, NODES)


def spread(field, tables):
    tile_set, slot_rows, slot_cols, live = tables
    width = field.shape[0]
    panels = field.reshape(width, N_NODE, RB, BLOCK)
    block_ids = jnp.arange(RB, dtype=jnp.int32)

    def target(part):
        total = jnp.zeros((width, RB, BLOCK), jnp.float32)
        for offset in range(OFFS):
            source = (part - offset + REACH) % N_NODE
            panel = jnp.take(panels, source, axis=1)
            pieces = jnp.take(panel, slot_rows[source, offset], axis=1)
            partial_out = jnp.einsum('hsr,srk->hsk', pieces.astype(jnp.float32), tile_set[source, offset].astype(jnp.float32), precision=lax.Precision.HIGHEST)
            selector = ((slot_cols[source, offset][None, :] == block_ids[:, None]) & live[source, offset][None, :]).astype(jnp.float32)
            total = total + jnp.einsum('hsk,bs->hbk', partial_out, selector, precision=lax.Precision.HIGHEST)
        return total

    stacked = lax.map(target, jnp.arange(N_NODE, dtype=jnp.int32))
    return jnp.transpose(stacked, (1, 0, 2, 3)).reshape(width, NODES)


def reference(features, tiles, tile_rows, tile_cols, counts, weight_one, weight_two, cotangent):
    tables = tile_tables(tiles, tile_rows, tile_cols, counts)
    first_agg = aggregate(features, tables).astype(jnp.bfloat16)
    first_pre = jnp.dot(weight_one.T, first_agg, preferred_element_type=jnp.float32)
    first_act = jax.nn.silu(first_pre).astype(jnp.bfloat16)
    second_agg = aggregate(first_act, tables).astype(jnp.bfloat16)
    layer_out = jnp.dot(weight_two.T, second_agg, preferred_element_type=jnp.float32).astype(jnp.bfloat16)
    weight_two_grad = jnp.dot(second_agg, cotangent.T, preferred_element_type=jnp.float32)
    second_back = jnp.dot(weight_two, cotangent, preferred_element_type=jnp.float32).astype(jnp.bfloat16)
    act_back = spread(second_back, tables).astype(jnp.bfloat16)
    sigma = jax.nn.sigmoid(first_pre)
    pre_back = (act_back.astype(jnp.float32) * sigma * (1.0 + first_pre * (1.0 - sigma))).astype(jnp.bfloat16)
    weight_one_grad = jnp.dot(first_agg, pre_back.T, preferred_element_type=jnp.float32)
    first_back = jnp.dot(weight_one, pre_back, preferred_element_type=jnp.float32).astype(jnp.bfloat16)
    feature_grad = spread(first_back, tables).astype(jnp.bfloat16)
    return (layer_out, feature_grad, weight_one_grad, weight_two_grad)
```

```python
import functools

import jax
import jax.numpy as jnp
from jax import lax
from jax.experimental import pallas as pl
from jax.experimental.pallas import tpu as pltpu
from jax.sharding import PartitionSpec as P

GROUP = 8
VMEM = pl.BlockSpec(memory_space=pltpu.VMEM)
SMEM = pl.BlockSpec(memory_space=pltpu.SMEM)
ANY = pl.BlockSpec(memory_space=pl.ANY)


def load_tiles(tiles_ref, buf, sems, slots, offsets):
    return [
        pltpu.make_async_copy(
            tiles_ref.at[pl.ds(o * slots, slots)],
            buf.at[pl.ds(o * slots, slots)],
            sems.at[o],
        )
        for o in range(offsets)
    ]


def accumulate(o, slots, counts, take, give, source, buf, target, block, spare, transposed):
    count = counts[o]
    contract = (((1,), (1,)), ((), ())) if transposed else (((1,), (0,)), ((), ()))

    def step(g, carry):
        parts = []
        for i in range(GROUP):
            s = g * GROUP + i
            t = o * slots + s
            c = pl.multiple_of(take[t] * block, block)
            product = lax.dot_general(
                source[:, pl.ds(c, block)],
                buf[t],
                contract,
                preferred_element_type=jnp.float32,
            )
            r = jnp.where(s < count, give[t], spare)
            parts.append((pl.multiple_of(r * block, block), product))
        for r, product in parts:
            target[:, pl.ds(r, block)] += product
        return carry

    lax.fori_loop(0, (count + GROUP - 1) // GROUP, step, 0)


def forward_kernel(slots, block, rows, cols, counts, *refs):
    offsets = counts.shape[0]
    panels = refs[:offsets]
    tiles_ref, out_ref, buf, acc, sems = refs[offsets:]
    width = out_ref.shape[1]
    copies = load_tiles(tiles_ref, buf, sems, slots, offsets)
    for copy in copies:
        copy.start()
    acc[...] = jnp.zeros_like(acc)
    for o in range(offsets):
        copies[o].wait()
        accumulate(
            o, slots, counts, cols, rows, panels[o], buf, acc, block, width // block, True
        )
    out_ref[...] = acc[:, :width].astype(out_ref.dtype)


def backward_kernel(slots, block, rows, cols, counts, panel, tiles_ref, *refs):
    offsets = counts.shape[0]
    outs = refs[:offsets]
    buf, acc, sems = refs[offsets:]
    width = panel.shape[1]
    copies = load_tiles(tiles_ref, buf, sems, slots, offsets)
    for copy in copies:
        copy.start()
    for o in range(offsets):
        acc[...] = jnp.zeros_like(acc)
        copies[o].wait()
        accumulate(
            o, slots, counts, rows, cols, panel, buf, acc, block, width // block, False
        )
        outs[o][...] = acc[:, :width].astype(outs[o].dtype)


def dense_kernel(agg, spread, one, two, one_t, two_t, out, back, one_grad, two_grad):
    f32 = functools.partial(jnp.dot, preferred_element_type=jnp.float32)
    tail = (((1,), (1,)), ((), ()))
    pre = f32(one_t[...], agg[...])
    sigma = 1.0 / (1.0 + jnp.exp(-pre))
    act = (pre * sigma).astype(jnp.bfloat16)
    out[...] = f32(two_t[...], act).astype(jnp.bfloat16)
    two_grad[...] = lax.dot_general(
        act, spread[...], tail, preferred_element_type=jnp.float32
    ).astype(two_grad.dtype)
    act_back = f32(two[...], spread[...]).astype(jnp.bfloat16).astype(jnp.float32)
    pre_back = (act_back * sigma * (1.0 + pre * (1.0 - sigma))).astype(jnp.bfloat16)
    back[...] = f32(one[...], pre_back).astype(jnp.bfloat16)
    one_grad[...] = lax.dot_general(
        agg[...], pre_back, tail, preferred_element_type=jnp.float32
    ).astype(one_grad.dtype)


def passed_along(value, axis, steps):
    count = lax.axis_size(axis)
    pairs = [(source, (source + steps) % count) for source in range(count)]
    return lax.ppermute(value, axis, pairs)


def on_device(features, tiles, tile_rows, tile_cols, counts, weight_one, weight_two, cotangent):
    offsets = counts.shape[0]
    reach = (offsets - 1) // 2
    slots = tile_rows.shape[0] // offsets
    block = tiles.shape[-1]
    height, width = features.shape
    depth = weight_one.shape[0]
    share = width // lax.axis_size("feat")
    limit = pltpu.CompilerParams(vmem_limit_bytes=48 << 20)
    bf16, f32 = jnp.bfloat16, jnp.float32
    scratch = [
        pltpu.VMEM(tiles.shape, tiles.dtype),
        pltpu.VMEM((height, width + block), f32),
        pltpu.SemaphoreType.DMA((offsets,)),
    ]
    cost = pl.CostEstimate(
        flops=2 * tiles.size * height, bytes_accessed=tiles.size * 2, transcendentals=0
    )

    def forward(panel):
        panels = [
            panel if o == reach else passed_along(panel, "node", reach - o)
            for o in range(offsets)
        ]
        return pl.pallas_call(
            functools.partial(forward_kernel, slots, block),
            out_shape=jax.ShapeDtypeStruct((height, width), bf16),
            in_specs=[SMEM] * 3 + [VMEM] * offsets + [ANY],
            out_specs=VMEM,
            scratch_shapes=scratch,
            compiler_params=limit,
            cost_estimate=cost,
        )(tile_rows, tile_cols, counts, *panels, tiles)

    def backward(panel):
        parts = pl.pallas_call(
            functools.partial(backward_kernel, slots, block),
            out_shape=[
                jax.ShapeDtypeStruct((height, width), f32 if o == reach else bf16)
                for o in range(offsets)
            ],
            in_specs=[SMEM] * 3 + [VMEM, ANY],
            out_specs=[VMEM] * offsets,
            scratch_shapes=scratch,
            compiler_params=limit,
            cost_estimate=cost,
        )(tile_rows, tile_cols, counts, panel, tiles)
        total = parts[reach]
        for o in range(offsets):
            if o != reach:
                total = total + passed_along(parts[o], "node", o - reach).astype(f32)
        return total.astype(bf16)

    def to_rows(field):
        return lax.all_to_all(field, "feat", split_axis=1, concat_axis=0, tiled=True)

    def to_features(field):
        return lax.all_to_all(field, "feat", split_axis=0, concat_axis=1, tiled=True)

    agg = to_rows(forward(features))
    spread = to_rows(backward(cotangent))
    out, back, one_part, two_part = pl.pallas_call(
        dense_kernel,
        out_shape=[jax.ShapeDtypeStruct((depth, share), bf16)] * 2
        + [jax.ShapeDtypeStruct((depth, depth), bf16)] * 2,
        in_specs=[VMEM] * 6,
        out_specs=[VMEM] * 4,
        compiler_params=limit,
    )(agg, spread, weight_one, weight_two, weight_one.T, weight_two.T)
    layer_out = forward(to_features(out))
    feature_grad = backward(to_features(back))

    grads = jnp.stack([one_part, two_part])
    feats, nodes = lax.axis_size("feat"), lax.axis_size("node")
    grads = lax.all_to_all(
        grads.reshape(2, feats, depth // feats, depth), "feat", split_axis=1, concat_axis=1
    )
    grads = jnp.sum(grads.astype(f32), axis=1)
    grads = lax.all_to_all(
        grads.reshape(nodes, -1, depth), "node", split_axis=0, concat_axis=0
    )
    grads = jnp.sum(grads, axis=0)
    grads = lax.all_gather(grads, "node", axis=0).reshape(2, depth // feats, depth)
    return (layer_out, feature_grad, grads[0], grads[1])


def solution(mesh):
    in_specs = (
        P("feat", "node"),
        P("node", None, None),
        P("node"),
        P("node"),
        P("node"),
        P(),
        P(),
        P("feat", "node"),
    )
    out_specs = (P("feat", "node"), P("feat", "node"), P("feat", None), P("feat", None))
    return jax.shard_map(
        on_device, mesh=mesh, in_specs=in_specs, out_specs=out_specs, check_vma=False
    )
```

```python
import functools

import jax
import jax.numpy as jnp
from jax import lax
from jax.experimental import pallas as pl
from jax.experimental.pallas import tpu as pltpu
from jax.sharding import PartitionSpec as P

GROUP = 8
CHUNKS = 2
MESH = pl.DeviceIdType.MESH
VMEM = pl.BlockSpec(memory_space=pltpu.VMEM)
SMEM = pl.BlockSpec(memory_space=pltpu.SMEM)
ANY = pl.BlockSpec(memory_space=pl.ANY)
TAIL = (((1,), (1,)), ((), ()))
BF16, F32 = jnp.bfloat16, jnp.float32


class Copies:
    def __init__(self, sent, landed):
        self.sent, self.landed, self.used = sent, landed, 0
        self.all = []

    def make(self, src, dst, node, feat):
        k = self.used
        self.used += 1
        copy = pltpu.make_async_remote_copy(
            src_ref=src,
            dst_ref=dst,
            send_sem=self.sent.at[k],
            recv_sem=self.landed.at[k],
            device_id=(node, feat),
            device_id_type=MESH,
        )
        self.all.append(copy)
        copy.start()
        return copy


def kernel(shape, *refs):
    slots, block, offsets, nodes, feats = shape
    (
        table, features, cotangent, tiles, weight_one, weight_two,
        layer_out, feature_grad, one_out, two_out,
        tile, chain_f, chain_b, feat_flat, cot_flat, feat_v, cot_v, one, two,
        sib_1, za_1, zd_1, relay_1, sib_2, za_2, zd_2, relay_2,
        out_1, out_2, comb_1, comb_2, got_1, got_2, own_1, own_2,
        agg_send, spread_send, agg, spread, up_send, back_send, up, back,
        pre_v, act_v, grads, got_grads, half, swapped, pieces, final, final_sib,
        local, sent, landed,
    ) = refs
    height, width = feat_flat.shape
    total_slots = offsets * slots
    blocks = width // block
    depth = agg.shape[0]
    share = agg.shape[1]
    ROWS, COLS, PREV_F, PREV_B = (k * total_slots for k in range(4))
    LAST_F = 4 * total_slots
    LAST_B = LAST_F + offsets * blocks
    none = total_slots

    me, mine = lax.axis_index("node"), lax.axis_index("feat")
    core = lax.rem(me, 2)
    sib = me + 1 - 2 * core
    ahead = lax.rem(me + 2 - 4 * core + nodes, nodes)
    behind = lax.rem(me - 2 + 4 * core + nodes, nodes)
    remote = Copies(sent, landed)

    loads = []
    for src, dst in (
        [(features, feat_flat), (cotangent, cot_flat)]
        + [
            (tiles.at[pl.ds(o * slots, slots)], tile.at[pl.ds(o * slots, slots)])
            for o in range(offsets)
        ]
        + [(weight_one, one), (weight_two, two)]
    ):
        copy = pltpu.make_async_copy(src, dst, local.at[len(loads)])
        copy.start()
        loads.append(copy)

    barrier = pltpu.get_barrier_semaphore()
    half_nodes = nodes // 2

    def greet(node, feat):
        pl.semaphore_signal(barrier, inc=1, device_id=(node, feat), device_id_type=MESH)

    greet(sib, mine)
    for d in range(1, half_nodes):
        greet(lax.rem(me + 2 * d, nodes), mine)
    for d in range(1, feats):
        greet(me, lax.rem(mine + d, feats))
    pl.semaphore_wait(barrier, half_nodes + feats - 1)

    def send_panel(panel, za, zd, sb):
        rows = blocks // CHUNKS
        parts = [
            remote.make(
                panel.at[pl.ds(k * rows, rows)], zd.at[pl.ds(k * rows, rows)], behind, mine
            )
            for k in range(CHUNKS)
        ]
        a = remote.make(panel, za, ahead, mine)
        s = remote.make(panel, sb, sib, mine)
        return parts, a, s

    def pass_on(parts, zd, relay):
        rows = blocks // CHUNKS
        relays = []
        for k, part in enumerate(parts):
            part.wait_recv()
            relays.append(
                remote.make(
                    zd.at[pl.ds(k * rows, rows)], relay.at[pl.ds(k * rows, rows)], sib, mine
                )
            )
        return relays

    def products(panel, o, take, prev, chain, contract):
        def step(g, carry):
            parts = []
            for i in range(GROUP):
                t = o * slots + g * GROUP + i
                parts.append(
                    lax.dot_general(
                        panel[table[take + t]],
                        tile[t],
                        contract,
                        preferred_element_type=F32,
                    )
                )
            for i in range(GROUP):
                t = o * slots + g * GROUP + i
                chain[t] = parts[i] + chain[table[prev + t]]
            return carry

        lax.fori_loop(0, slots // GROUP, step, 0)

    def forward(panel, o):
        products(panel, o, COLS, PREV_F, chain_f, TAIL)

    def gather_forward(out):
        def step(r, carry):
            total = chain_f[table[LAST_F + r]]
            for o in range(1, offsets):
                total = total + chain_f[table[LAST_F + o * blocks + r]]
            out[:, pl.ds(pl.multiple_of(r * block, block), block)] = total.astype(out.dtype)
            return carry

        lax.fori_loop(0, blocks, step, 0)

    def backward(panel, o, out):
        products(panel, o, ROWS, PREV_B, chain_b, (((1,), (0,)), ((), ())))

        def step(r, carry):
            part = chain_b[table[LAST_B + o * blocks + r]]
            out[:, pl.ds(pl.multiple_of(r * block, block), block)] = part.astype(out.dtype)
            return carry

        lax.fori_loop(0, blocks, step, 0)

    def spread_out(panel, out, comb, got, own):
        p_dir, p_comb, p_add, p_sib = (out.at[k] for k in range(4))
        backward(panel, 4 * core, p_dir)
        c_dir = remote.make(p_dir, got.at[0], behind, mine)
        backward(panel, 1 + 2 * core, p_comb)
        c_comb = remote.make(p_comb, comb, sib, mine)
        backward(panel, 4 - 4 * core, p_add)
        c_comb.wait_recv()
        p_add[...] = (p_add[...].astype(F32) + comb[...].astype(F32)).astype(BF16)
        c_add = remote.make(p_add, got.at[1], ahead, mine)
        backward(panel, 3 - 2 * core, p_sib)
        c_sib = remote.make(p_sib, got.at[2], sib, mine)
        backward(panel, 2, own)
        return c_dir, c_add, c_sib

    def collect(copies, got, own, out):
        for copy in copies:
            copy.wait_recv()
        total = own[...]
        for k in range(3):
            total = total + got[k].astype(F32)
        out[...] = total.astype(out.dtype)

    def rows_of(k):
        return pl.ds(pl.multiple_of(k * height, height), height)

    def columns_of(k):
        return pl.ds(pl.multiple_of(k * share, share), share)

    def to_rows(src, dst):
        copies = []
        for d in range(1, feats):
            peer = lax.rem(mine + d, feats)
            copies.append(
                remote.make(src.at[:, columns_of(peer)], dst.at[rows_of(mine)], me, peer)
            )
        dst[rows_of(mine)] = src[:, columns_of(mine)]
        return copies

    def to_features(src, dst):
        kept = share // block
        place = pl.ds(mine * kept, kept)
        copies = []
        for d in range(1, feats):
            peer = lax.rem(mine + d, feats)
            copies.append(remote.make(src.at[:, rows_of(peer)], dst.at[place], me, peer))
        dst[place] = src[:, rows_of(mine)]
        return copies

    def by_blocks(flat, panel):
        def step(r, carry):
            panel[r] = flat[:, pl.ds(pl.multiple_of(r * block, block), block)]
            return carry

        lax.fori_loop(0, blocks, step, 0)

    def put_blocks(value, out):
        for k in range(share // block):
            out[k] = value[:, k * block : (k + 1) * block]

    def arrived(copies):
        for copy in copies:
            copy.wait_recv()

    loads[0].wait()
    by_blocks(feat_flat, feat_v)
    parts, c_za, c_sb = send_panel(feat_v, za_1, zd_1, sib_1)
    chain_f[none] = jnp.zeros(chain_f.shape[1:], F32)
    chain_b[none] = jnp.zeros(chain_b.shape[1:], F32)
    loads[1].wait()
    by_blocks(cot_flat, cot_v)
    for copy in loads[2 : offsets + 2]:
        copy.wait()
    sums = spread_out(cot_v, out_1, comb_1, got_1, own_1)
    forward(feat_v, 2)
    c_sb.wait_recv()
    forward(sib_1, 3 - 2 * core)
    relays = pass_on(parts, zd_1, relay_1)
    forward(zd_1, 4 - 4 * core)
    c_za.wait_recv()
    forward(za_1, 4 * core)
    arrived(relays)
    forward(relay_1, 1 + 2 * core)
    gather_forward(agg_send)
    agg_copies = to_rows(agg_send, agg)
    collect(sums, got_1, own_1, spread_send)
    spread_copies = to_rows(spread_send, spread)

    dot = functools.partial(jnp.dot, preferred_element_type=F32)
    lead = (((0,), (0,)), ((), ()))
    loads[offsets + 2].wait()
    loads[offsets + 3].wait()
    arrived(agg_copies)
    pre = lax.dot_general(one[...], agg[...], lead, preferred_element_type=F32)
    pre_v[...] = pre
    act_v[...] = (pre * (1.0 / (1.0 + jnp.exp(-pre)))).astype(BF16)
    put_blocks(
        lax.dot_general(two[...], act_v[...], lead, preferred_element_type=F32).astype(BF16),
        up_send,
    )
    up_copies = to_features(up_send, up)
    arrived(spread_copies)
    act_back = dot(two[...], spread[...]).astype(BF16).astype(F32)
    pre = pre_v[...]
    sigma = 1.0 / (1.0 + jnp.exp(-pre))
    pre_back = (act_back * sigma * (1.0 + pre * (1.0 - sigma))).astype(BF16)
    put_blocks(dot(one[...], pre_back).astype(BF16), back_send)
    back_copies = to_features(back_send, back)
    grads[0] = lax.dot_general(agg[...], pre_back, TAIL, preferred_element_type=F32).astype(BF16)
    arrived(up_copies)
    parts, c_za, c_sb = send_panel(up, za_2, zd_2, sib_2)
    grads[1] = lax.dot_general(
        act_v[...], spread[...], TAIL, preferred_element_type=F32
    ).astype(BF16)

    arrived(back_copies)
    sums = spread_out(back, out_2, comb_2, got_2, own_2)
    grad_copies = []
    for d in range(1, feats):
        peer = lax.rem(mine + d, feats)
        grad_copies.append(
            remote.make(grads.at[:, rows_of(peer)], got_grads.at[d - 1], me, peer)
        )
    forward(up, 2)
    c_sb.wait_recv()
    forward(sib_2, 3 - 2 * core)
    relays = pass_on(parts, zd_2, relay_2)
    arrived(grad_copies)
    total = grads[:, rows_of(mine)].astype(F32)
    for d in range(feats - 1):
        total = total + got_grads[d].astype(F32)
    half[...] = total
    swap = remote.make(half.at[1 - core], swapped, sib, mine)
    forward(zd_2, 4 - 4 * core)
    swap.wait_recv()
    swapped[...] = swapped[...] + half[core]
    groups = min(half_nodes, height // 8)
    splits = half_nodes // groups
    tall, wide = height // groups, depth // splits

    def piece(k):
        row, column = k // splits, lax.rem(k, splits)
        return (
            pl.ds(pl.multiple_of(row * tall, tall), tall),
            pl.ds(pl.multiple_of(column * wide, wide), wide),
        )

    place = me // 2
    piece_copies = []
    for d in range(1, half_nodes):
        peer = lax.rem(place + d, half_nodes)
        piece_copies.append(
            remote.make(
                swapped.at[piece(peer)], pieces.at[d - 1], 2 * peer + core, mine
            )
        )
    c_za.wait_recv()
    forward(za_2, 4 * core)
    arrived(piece_copies)
    total = swapped[piece(place)]
    for d in range(half_nodes - 1):
        total = total + pieces[d]
    final[piece(place)] = total
    final_copies = []
    for d in range(1, half_nodes):
        peer = lax.rem(place + d, half_nodes)
        final_copies.append(
            remote.make(
                final.at[piece(place)], final.at[piece(place)], 2 * peer + core, mine
            )
        )
    arrived(relays)
    forward(relay_2, 1 + 2 * core)
    gather_forward(layer_out)
    arrived(final_copies)
    last = remote.make(final, final_sib, sib, mine)
    collect(sums, got_2, own_2, feature_grad)
    last.wait_recv()

    @pl.when(core == 0)
    def _():
        one_out[...] = final[...]
        two_out[...] = final_sib[...]

    @pl.when(core == 1)
    def _():
        one_out[...] = final_sib[...]
        two_out[...] = final[...]

    for copy in remote.all:
        copy.wait_send()


def links(keys, live, blocks):
    offsets, slots = keys.shape
    place = jnp.arange(slots, dtype=jnp.int32)
    base = (jnp.arange(offsets, dtype=jnp.int32) * slots)[:, None]
    none = offsets * slots
    same = (keys[:, :, None] == keys[:, None, :]) & (place[None, :, None] > place[None, None, :])
    prev = jnp.max(jnp.where(same, place[None, None, :], -1), axis=2)
    owns = (keys[:, None, :] == jnp.arange(blocks, dtype=jnp.int32)[None, :, None]) & live[
        :, None, :
    ]
    last = jnp.max(jnp.where(owns, place[None, None, :], -1), axis=2)
    return jnp.where(prev < 0, none, prev + base), jnp.where(last < 0, none, last + base)


def on_device(features, tiles, tile_rows, tile_cols, counts, weight_one, weight_two, cotangent):
    offsets = counts.shape[0]
    slots = tile_rows.shape[0] // offsets
    block = tiles.shape[-1]
    height, width = features.shape
    depth = weight_one.shape[0]
    nodes, feats = lax.axis_size("node"), lax.axis_size("feat")
    share = width // feats
    rows, cols = tile_rows.reshape(offsets, slots), tile_cols.reshape(offsets, slots)
    live = jnp.arange(slots, dtype=jnp.int32)[None, :] < counts[:, None]
    prev_f, last_f = links(rows, live, width // block)
    prev_b, last_b = links(cols, live, width // block)
    table = jnp.concatenate(
        [t.reshape(-1) for t in (rows, cols, prev_f, prev_b, last_f, last_b)]
    )
    half_nodes = nodes // 2
    groups = min(half_nodes, height // 8)
    piece = (height // groups, depth * groups // half_nodes)
    remote_copies = 2 * (4 + 2 * CHUNKS - 2 + 4) + 5 * (feats - 1) + 2 + 2 * (half_nodes - 1)
    flat = pltpu.VMEM((height, width), BF16)
    panel = pltpu.VMEM((width // block, height, block), BF16)
    stack = pltpu.VMEM((share // block, depth, block), BF16)
    chain = pltpu.VMEM((offsets * slots + 1, height, block), F32)
    square = pltpu.VMEM((depth, depth), BF16)
    side = pltpu.VMEM((depth, share), BF16)
    return pl.pallas_call(
        functools.partial(kernel, (slots, block, offsets, nodes, feats)),
        out_shape=[jax.ShapeDtypeStruct((height, width), BF16)] * 2
        + [jax.ShapeDtypeStruct((height, depth), F32)] * 2,
        in_specs=[SMEM] + [ANY] * 5,
        out_specs=[VMEM] * 4,
        scratch_shapes=[pltpu.VMEM(tiles.shape, BF16), chain, chain]
        + [flat, flat, panel, panel, square, square]
        + [panel] * 8
        + [pltpu.VMEM((4, height, width), BF16)] * 2
        + [flat] * 2
        + [pltpu.VMEM((3, height, width), BF16)] * 2
        + [pltpu.VMEM((height, width), F32)] * 2
        + [flat, flat, side, side, stack, stack, panel, panel]
        + [
            pltpu.VMEM((depth, share), F32),
            side,
            pltpu.VMEM((2, depth, depth), BF16),
            pltpu.VMEM((feats - 1, 2, height, depth), BF16),
            pltpu.VMEM((2, height, depth), F32),
            pltpu.VMEM((height, depth), F32),
            pltpu.VMEM((half_nodes - 1, *piece), F32),
            pltpu.VMEM((height, depth), F32),
            pltpu.VMEM((height, depth), F32),
            pltpu.SemaphoreType.DMA((offsets + 4,)),
            pltpu.SemaphoreType.DMA((remote_copies,)),
            pltpu.SemaphoreType.DMA((remote_copies,)),
        ],
        compiler_params=pltpu.CompilerParams(
            collective_id=0, has_side_effects=True, vmem_limit_bytes=60 << 20
        ),
    )(table, features, cotangent, tiles, weight_one, weight_two)


def solution(mesh):
    in_specs = (
        P("feat", "node"),
        P("node", None, None),
        P("node"),
        P("node"),
        P("node"),
        P(),
        P(),
        P("feat", "node"),
    )
    out_specs = (P("feat", "node"), P("feat", "node"), P("feat", None), P("feat", None))
    return jax.shard_map(
        on_device, mesh=mesh, in_specs=in_specs, out_specs=out_specs, check_vma=False
    )
```

```python
import functools

import jax
import jax.numpy as jnp
from jax import lax
from jax.experimental import pallas as pl
from jax.experimental.pallas import tpu as pltpu
from jax.sharding import PartitionSpec as P

GROUP = 8
CHUNKS = 2
SIDES = 2
MESH = pl.DeviceIdType.MESH
VMEM = pl.BlockSpec(memory_space=pltpu.VMEM)
SMEM = pl.BlockSpec(memory_space=pltpu.SMEM)
ANY = pl.BlockSpec(memory_space=pl.ANY)
TAIL = (((1,), (1,)), ((), ()))
BF16, F32 = jnp.bfloat16, jnp.float32


class Copy:
    def __init__(self, copy):
        self.copy, self.left = copy, False
        copy.start()

    def wait_recv(self):
        self.copy.wait_recv()

    def wait_send(self):
        if not self.left:
            self.copy.wait_send()
        self.left = True


class Copies:
    def __init__(self, sent, landed):
        self.sent, self.landed, self.all = sent, landed, []

    def make(self, src, dst, node, feat):
        k = len(self.all)
        copy = Copy(
            pltpu.make_async_remote_copy(
                src_ref=src,
                dst_ref=dst,
                send_sem=self.sent.at[k],
                recv_sem=self.landed.at[k],
                device_id=(node, feat),
                device_id_type=MESH,
            )
        )
        self.all.append(copy)
        return copy


def table_kernel(slots, blocks, counts, rows_v, cols_v, table_v):
    offsets, total = counts.shape[0], rows_v.shape[1]
    iota = functools.partial(lax.broadcasted_iota, jnp.int32)
    down, along = iota((total, total), 0), iota((total, total), 1)

    def place(index, size, count):
        group = jnp.zeros_like(index)
        for k in range(1, count):
            group = group + (index >= k * size).astype(jnp.int32)
        return group

    close = (down < along) & (place(down, slots, offsets) == place(along, slots, offsets))
    line = iota((total, 1), 0)
    owner = place(line, slots, offsets)
    limit = jnp.zeros_like(line)
    for o in range(offsets):
        limit = jnp.where(owner == o, o * slots + counts[o], limit)
    spots = iota((1, offsets * blocks), 1)
    group = place(spots, blocks, offsets)
    for keys_v, prev, last in ((rows_v, 0, 2), (cols_v, 1, 3)):
        keys = keys_v[...].astype(F32)
        column = jnp.sum(jnp.where(down == along, keys, 0.0), axis=1, keepdims=True)
        where = jnp.max(
            jnp.where(close & (column == keys), down.astype(F32), -1.0), axis=0, keepdims=True
        ).astype(jnp.int32)
        table_v[prev : prev + 1, :total] = jnp.where(where < 0, total, where)
        wanted = (spots - group * blocks).astype(F32)
        mine = (column == wanted) & (owner == group) & (line < limit)
        where = jnp.max(
            jnp.where(mine, line.astype(F32), -1.0), axis=0, keepdims=True
        ).astype(jnp.int32)
        table_v[last : last + 1, : offsets * blocks] = jnp.where(where < 0, total, where)


def kernel(shape, *refs):
    slots, block, offsets, nodes, feats = shape
    (
        rows, cols, table, features, cotangent, tiles, weight_one, weight_two,
        layer_out, feature_grad, one_out, two_out,
        tile, chain_f, chain_b, feat_flat, cot_flat, feat_v, cot_v, one, two,
        sib_1, za_1, zd_1, relay_1, sib_2, za_2, zd_2, relay_2,
        out_1, out_2, comb_1, comb_2, got_1, got_2, own_1, own_2,
        agg_send, spread_send, agg, spread, up_send, back_send, up, back,
        pre_v, act_v, grads, grad_sib, grad_chip, got_y, half, swapped, pieces, final, final_sib,
        local, sent, landed,
    ) = refs
    height, width = feat_flat.shape
    total_slots = offsets * slots
    blocks = width // block
    depth = agg.shape[0]
    share = agg.shape[1]
    PREV_F, PREV_B, LAST_F, LAST_B = range(4)
    none = total_slots

    me, mine = lax.axis_index("node"), lax.axis_index("feat")
    core = lax.rem(me, 2)
    sib = me + 1 - 2 * core
    ahead = lax.rem(me + 2 - 4 * core + nodes, nodes)
    behind = lax.rem(me - 2 + 4 * core + nodes, nodes)
    remote = Copies(sent, landed)

    loads = []
    for src, dst in (
        [(features, feat_flat), (cotangent, cot_flat)]
        + [
            (tiles.at[pl.ds(o * slots, slots)], tile.at[pl.ds(o * slots, slots)])
            for o in range(offsets)
        ]
        + [(weight_one, one), (weight_two, two)]
    ):
        copy = pltpu.make_async_copy(src, dst, local.at[len(loads)])
        copy.start()
        loads.append(copy)

    def by_blocks(flat, panel):
        def step(r, carry):
            panel[r] = flat[:, pl.ds(pl.multiple_of(r * block, block), block)]
            return carry

        lax.fori_loop(0, blocks, step, 0)

    barrier = pltpu.get_barrier_semaphore()
    half_nodes = nodes // 2

    def greet(node, feat):
        pl.semaphore_signal(barrier, inc=1, device_id=(node, feat), device_id_type=MESH)

    greet(sib, mine)
    for d in range(1, half_nodes):
        greet(lax.rem(me + 2 * d, nodes), mine)
    for d in range(1, feats):
        greet(me, lax.rem(mine + d, feats))
    loads[0].wait()
    by_blocks(feat_flat, feat_v)
    pl.semaphore_wait(barrier, half_nodes + feats - 1)

    def send_panel(panel, za, zd, sb):
        rows = blocks // CHUNKS
        parts = [
            remote.make(
                panel.at[pl.ds(k * rows, rows)], zd.at[pl.ds(k * rows, rows)], behind, mine
            )
            for k in range(CHUNKS)
        ]
        a = remote.make(panel, za, ahead, mine)
        s = remote.make(panel, sb, sib, mine)
        return parts, a, s

    def pass_on(parts, zd, relay):
        rows = blocks // CHUNKS
        relays = []
        for k, part in enumerate(parts):
            part.wait_recv()
            relays.append(
                remote.make(
                    zd.at[pl.ds(k * rows, rows)], relay.at[pl.ds(k * rows, rows)], sib, mine
                )
            )
        return relays

    def products(panel, o, take, prev, chain, contract):
        def step(g, carry):
            parts = []
            for i in range(GROUP):
                t = o * slots + g * GROUP + i
                parts.append(
                    lax.dot_general(
                        panel[take[t]],
                        tile[t],
                        contract,
                        preferred_element_type=F32,
                    )
                )
            for i in range(GROUP):
                t = o * slots + g * GROUP + i
                chain[t] = parts[i] + chain[table[prev, t]]
            return carry

        lax.fori_loop(0, slots // GROUP, step, 0)

    def forward(panel, o):
        products(panel, o, cols, PREV_F, chain_f, TAIL)

    def gather_forward(out):
        def step(r, carry):
            total = chain_f[table[LAST_F, r]]
            for o in range(1, offsets):
                total = total + chain_f[table[LAST_F, o * blocks + r]]
            out[:, pl.ds(pl.multiple_of(r * block, block), block)] = total.astype(out.dtype)
            return carry

        lax.fori_loop(0, blocks, step, 0)

    def backward(panel, o, out):
        products(panel, o, rows, PREV_B, chain_b, (((1,), (0,)), ((), ())))

        def step(r, carry):
            part = chain_b[table[LAST_B, o * blocks + r]]
            out[:, pl.ds(pl.multiple_of(r * block, block), block)] = part.astype(out.dtype)
            return carry

        lax.fori_loop(0, blocks, step, 0)

    def spread_early(panel, out, comb, got):
        p_dir, p_comb, p_add, p_sib = (out.at[k] for k in range(4))
        backward(panel, 1 + 2 * core, p_comb)
        c_comb = remote.make(p_comb, comb, sib, mine)
        backward(panel, 4 * core, p_dir)
        backward(panel, 4 - 4 * core, p_add)
        backward(panel, 3 - 2 * core, p_sib)
        return c_comb, remote.make(p_sib, got.at[2], sib, mine)

    def spread_late(before, c_comb, out, comb, got):
        parts, a = before
        p_dir, p_add = out.at[0], out.at[2]
        for part in parts:
            part.wait_send()
        c_dir = remote.make(p_dir, got.at[0], behind, mine)
        c_comb.wait_recv()
        p_add[...] = (p_add[...].astype(F32) + comb[...].astype(F32)).astype(BF16)
        a.wait_send()
        return c_dir, remote.make(p_add, got.at[1], ahead, mine)

    def collect(copies, got, own, out):
        for copy in copies:
            copy.wait_recv()
        total = own[...]
        for k in range(3):
            total = total + got[k].astype(F32)
        out[...] = total.astype(out.dtype)

    def rows_of(k):
        return pl.ds(pl.multiple_of(k * height, height), height)

    def columns_of(k):
        return pl.ds(pl.multiple_of(k * share, share), share)

    def to_rows(src, dst):
        copies = []
        for d in range(1, feats):
            peer = lax.rem(mine + d, feats)
            copies.append(
                remote.make(src.at[:, columns_of(peer)], dst.at[rows_of(mine)], me, peer)
            )
        dst[rows_of(mine)] = src[:, columns_of(mine)]
        return copies

    def to_features(src, dst):
        kept = share // block
        place = pl.ds(mine * kept, kept)
        copies = []
        for d in range(1, feats):
            peer = lax.rem(mine + d, feats)
            copies.append(remote.make(src.at[:, rows_of(peer)], dst.at[place], me, peer))
        dst[place] = src[:, rows_of(mine)]
        return copies

    def put_blocks(value, out):
        for k in range(share // block):
            out[k] = value[:, k * block : (k + 1) * block]

    def arrived(copies):
        for copy in copies:
            copy.wait_recv()

    parts, c_za, c_sb = send_panel(feat_v, za_1, zd_1, sib_1)
    chain_f[none] = jnp.zeros(chain_f.shape[1:], F32)
    chain_b[none] = jnp.zeros(chain_b.shape[1:], F32)
    loads[1].wait()
    by_blocks(cot_flat, cot_v)
    for copy in loads[2 : offsets + 2]:
        copy.wait()
    c_comb, c_own = spread_early(cot_v, out_1, comb_1, got_1)
    forward(feat_v, 2)
    c_sb.wait_recv()
    forward(sib_1, 3 - 2 * core)
    sums = (c_own, *spread_late((parts, c_za), c_comb, out_1, comb_1, got_1))
    relays = pass_on(parts, zd_1, relay_1)
    forward(zd_1, 4 - 4 * core)
    c_za.wait_recv()
    forward(za_1, 4 * core)
    arrived(relays)
    forward(relay_1, 1 + 2 * core)
    gather_forward(agg_send)
    agg_copies = to_rows(agg_send, agg)
    backward(cot_v, 2, own_1)
    collect(sums, got_1, own_1, spread_send)
    spread_copies = to_rows(spread_send, spread)

    dot = functools.partial(jnp.dot, preferred_element_type=F32)
    lead = (((0,), (0,)), ((), ()))
    loads[offsets + 2].wait()
    loads[offsets + 3].wait()
    arrived(agg_copies)
    pre = lax.dot_general(one[...], agg[...], lead, preferred_element_type=F32)
    pre_v[...] = pre
    act_v[...] = (pre * (1.0 / (1.0 + jnp.exp(-pre)))).astype(BF16)
    put_blocks(
        lax.dot_general(two[...], act_v[...], lead, preferred_element_type=F32).astype(BF16),
        up_send,
    )
    up_copies = to_features(up_send, up)
    arrived(spread_copies)
    act_back = dot(two[...], spread[...]).astype(BF16).astype(F32)
    pre = pre_v[...]
    sigma = 1.0 / (1.0 + jnp.exp(-pre))
    pre_back = (act_back * sigma * (1.0 + pre * (1.0 - sigma))).astype(BF16)
    put_blocks(dot(one[...], pre_back).astype(BF16), back_send)
    arrived(up_copies)
    parts, c_za, c_sb = send_panel(up, za_2, zd_2, sib_2)
    back_copies = to_features(back_send, back)
    grads[0] = lax.dot_general(agg[...], pre_back, TAIL, preferred_element_type=F32).astype(BF16)
    grads[1] = lax.dot_general(
        act_v[...], spread[...], TAIL, preferred_element_type=F32
    ).astype(BF16)
    c_grad = remote.make(grads.at[1 - core], grad_sib, sib, mine)

    forward(up, 2)
    c_grad.wait_recv()
    side = feats // SIDES * height
    added = grads[core].astype(F32) + grad_sib[...].astype(F32)
    for k in range(SIDES):
        grad_chip[k] = added[k * side : (k + 1) * side].astype(BF16)
    ring = feats // SIDES
    near, far = lax.rem(mine, ring), mine // ring
    arrived(back_copies)
    ring_copies = []
    for d in range(1, ring):
        peer = lax.rem(near + d, ring)
        ring_copies.append(
            remote.make(grad_chip.at[:, rows_of(peer)], got_y.at[d - 1], me, far * ring + peer)
        )
    p_dir, p_comb, p_add, p_sib = (out_2.at[k] for k in range(4))
    backward(back, 4 * core, p_dir)
    c_dir = remote.make(p_dir, got_2.at[0], behind, mine)
    backward(back, 1 + 2 * core, p_comb)
    c_comb = remote.make(p_comb, comb_2, sib, mine)
    backward(back, 4 - 4 * core, p_add)
    c_comb.wait_recv()
    p_add[...] = (p_add[...].astype(F32) + comb_2[...].astype(F32)).astype(BF16)
    c_add = remote.make(p_add, got_2.at[1], ahead, mine)
    arrived(ring_copies)
    total = grad_chip[:, rows_of(near)].astype(F32)
    for d in range(ring - 1):
        total = total + got_y[d].astype(F32)
    half[...] = total
    swap = remote.make(half.at[1 - far], swapped, me, (1 - far) * ring + near)
    backward(back, 3 - 2 * core, p_sib)
    sums = c_dir, c_add, remote.make(p_sib, got_2.at[2], sib, mine)
    relays = pass_on(parts, zd_2, relay_2)
    swap.wait_recv()
    swapped[...] = swapped[...] + half[far]
    groups = min(half_nodes, height // 8)
    splits = half_nodes // groups
    tall, wide = height // groups, depth // splits

    def piece(k):
        row, column = k // splits, lax.rem(k, splits)
        return (
            pl.ds(pl.multiple_of(row * tall, tall), tall),
            pl.ds(pl.multiple_of(column * wide, wide), wide),
        )

    place = me // 2
    piece_copies = []
    for d in range(1, half_nodes):
        peer = lax.rem(place + d, half_nodes)
        piece_copies.append(
            remote.make(
                swapped.at[piece(peer)], pieces.at[d - 1], 2 * peer + core, mine
            )
        )
    c_sb.wait_recv()
    forward(sib_2, 3 - 2 * core)
    arrived(piece_copies)
    total = swapped[piece(place)]
    for d in range(half_nodes - 1):
        total = total + pieces[d]
    final[piece(place)] = total
    final_copies = []
    for d in range(1, half_nodes):
        peer = lax.rem(place + d, half_nodes)
        final_copies.append(
            remote.make(
                final.at[piece(place)], final.at[piece(place)], 2 * peer + core, mine
            )
        )
    c_za.wait_recv()
    forward(za_2, 4 * core)
    forward(zd_2, 4 - 4 * core)
    arrived(final_copies)
    last = remote.make(final, final_sib, sib, mine)
    arrived(relays)
    forward(relay_2, 1 + 2 * core)
    gather_forward(layer_out)
    backward(back, 2, own_2)
    last.wait_recv()
    collect(sums, got_2, own_2, feature_grad)

    @pl.when(core == 0)
    def _():
        one_out[...] = final[...]
        two_out[...] = final_sib[...]

    @pl.when(core == 1)
    def _():
        one_out[...] = final_sib[...]
        two_out[...] = final[...]

    for copy in remote.all:
        copy.wait_send()


def give_kernel(*refs):
    half = (len(refs) - 1) // 2
    copies = [
        pltpu.make_async_copy(src, dst, refs[-1].at[k])
        for k, (src, dst) in enumerate(zip(refs[:half], refs[half:-1]))
    ]
    for copy in copies:
        copy.start()
    for copy in copies:
        copy.wait()


def on_device(features, tiles, tile_rows, tile_cols, counts, weight_one, weight_two, cotangent):
    offsets = counts.shape[0]
    slots = tile_rows.shape[0] // offsets
    block = tiles.shape[-1]
    height, width = features.shape
    depth = weight_one.shape[0]
    nodes, feats = lax.axis_size("node"), lax.axis_size("feat")
    share = width // feats
    lanes = -(-max(tile_rows.shape[0], offsets * (width // block)) // 128) * 128
    half_nodes = nodes // 2
    groups = min(half_nodes, height // 8)
    piece = (height // groups, depth * groups // half_nodes)
    remote_copies = (
        2 * (2 * CHUNKS + 6) + 4 * (feats - 1) + feats // SIDES - 1 + 3 + 2 * (half_nodes - 1)
    )
    flat = pltpu.VMEM((height, width), BF16)
    panel = pltpu.VMEM((width // block, height, block), BF16)
    stack = pltpu.VMEM((share // block, depth, block), BF16)
    chain = pltpu.VMEM((offsets * slots + 1, height, block), F32)
    square = pltpu.VMEM((depth, depth), BF16)
    side = pltpu.VMEM((depth, share), BF16)
    table = pl.pallas_call(
        functools.partial(table_kernel, slots, width // block),
        out_shape=jax.ShapeDtypeStruct((8, lanes), jnp.int32),
        in_specs=[SMEM, VMEM, VMEM],
        out_specs=VMEM,
    )(counts, tile_rows.reshape(1, -1), tile_cols.reshape(1, -1))
    made = pl.pallas_call(
        functools.partial(kernel, (slots, block, offsets, nodes, feats)),
        out_shape=[jax.ShapeDtypeStruct((height, width), BF16)] * 2
        + [jax.ShapeDtypeStruct((height, depth), F32)] * 2,
        in_specs=[SMEM] * 3 + [ANY] * 5,
        out_specs=[VMEM] * 4,
        scratch_shapes=[pltpu.VMEM(tiles.shape, BF16), chain, chain]
        + [flat, flat, panel, panel, square, square]
        + [panel] * 8
        + [pltpu.VMEM((4, height, width), BF16)] * 2
        + [flat] * 2
        + [pltpu.VMEM((3, height, width), BF16)] * 2
        + [pltpu.VMEM((height, width), F32)] * 2
        + [flat, flat, side, side, stack, stack, panel, panel]
        + [
            pltpu.VMEM((depth, share), F32),
            side,
            pltpu.VMEM((2, depth, depth), BF16),
            square,
            pltpu.VMEM((SIDES, depth // SIDES, depth), BF16),
            pltpu.VMEM((max(feats // SIDES - 1, 1), SIDES, height, depth), BF16),
            pltpu.VMEM((SIDES, height, depth), F32),
            pltpu.VMEM((height, depth), F32),
            pltpu.VMEM((half_nodes - 1, *piece), F32),
            pltpu.VMEM((height, depth), F32),
            pltpu.VMEM((height, depth), F32),
            pltpu.SemaphoreType.DMA((offsets + 4,)),
            pltpu.SemaphoreType.DMA((remote_copies,)),
            pltpu.SemaphoreType.DMA((remote_copies,)),
        ],
        compiler_params=pltpu.CompilerParams(
            collective_id=0, has_side_effects=True, vmem_limit_bytes=60 << 20
        ),
    )(
        tile_rows,
        tile_cols,
        table,
        features,
        cotangent,
        tiles,
        weight_one,
        weight_two,
    )
    return pl.pallas_call(
        give_kernel,
        out_shape=[jax.ShapeDtypeStruct(m.shape, m.dtype) for m in made],
        in_specs=[ANY] * 4,
        out_specs=[ANY] * 4,
        scratch_shapes=[pltpu.SemaphoreType.DMA((4,))],
    )(*made)


def solution(mesh):
    in_specs = (
        P("feat", "node"),
        P("node", None, None),
        P("node"),
        P("node"),
        P("node"),
        P(),
        P(),
        P("feat", "node"),
    )
    out_specs = (P("feat", "node"), P("feat", "node"), P("feat", None), P("feat", None))
    return jax.shard_map(
        on_device, mesh=mesh, in_specs=in_specs, out_specs=out_specs, check_vma=False
    )
```

```python
import functools

import jax
import jax.numpy as jnp
from jax import lax
from jax.experimental import pallas as pl
from jax.experimental.pallas import tpu as pltpu
from jax.sharding import PartitionSpec as P

GROUP = 8
CHUNKS = 2
SIDES = 2
MESH = pl.DeviceIdType.MESH
VMEM = pl.BlockSpec(memory_space=pltpu.VMEM)
SMEM = pl.BlockSpec(memory_space=pltpu.SMEM)
ANY = pl.BlockSpec(memory_space=pl.ANY)
TAIL = (((1,), (1,)), ((), ()))
BF16, F32 = jnp.bfloat16, jnp.float32


class Copy:
    def __init__(self, copy):
        self.copy, self.left = copy, False
        copy.start()

    def wait_recv(self):
        self.copy.wait_recv()

    def wait_send(self):
        if not self.left:
            self.copy.wait_send()
        self.left = True


class Copies:
    def __init__(self, sent, landed):
        self.sent, self.landed, self.all = sent, landed, []

    def make(self, src, dst, node, feat):
        k = len(self.all)
        copy = Copy(
            pltpu.make_async_remote_copy(
                src_ref=src,
                dst_ref=dst,
                send_sem=self.sent.at[k],
                recv_sem=self.landed.at[k],
                device_id=(node, feat),
                device_id_type=MESH,
            )
        )
        self.all.append(copy)
        return copy


def table_kernel(slots, blocks, counts, rows_v, cols_v, table_v):
    offsets, total = counts.shape[0], rows_v.shape[1]
    iota = functools.partial(lax.broadcasted_iota, jnp.int32)
    down, along = iota((total, total), 0), iota((total, total), 1)

    def place(index, size, count):
        group = jnp.zeros_like(index)
        for k in range(1, count):
            group = group + (index >= k * size).astype(jnp.int32)
        return group

    close = (down < along) & (place(down, slots, offsets) == place(along, slots, offsets))
    line = iota((total, 1), 0)
    owner = place(line, slots, offsets)
    limit = jnp.zeros_like(line)
    for o in range(offsets):
        limit = jnp.where(owner == o, o * slots + counts[o], limit)
    spots = iota((1, offsets * blocks), 1)
    group = place(spots, blocks, offsets)
    for keys_v, prev, last in ((rows_v, 0, 2), (cols_v, 1, 3)):
        keys = keys_v[...].astype(F32)
        column = jnp.sum(jnp.where(down == along, keys, 0.0), axis=1, keepdims=True)
        where = jnp.max(
            jnp.where(close & (column == keys), down.astype(F32), -1.0), axis=0, keepdims=True
        ).astype(jnp.int32)
        table_v[prev : prev + 1, :total] = jnp.where(where < 0, total, where)
        wanted = (spots - group * blocks).astype(F32)
        mine = (column == wanted) & (owner == group) & (line < limit)
        where = jnp.max(
            jnp.where(mine, line.astype(F32), -1.0), axis=0, keepdims=True
        ).astype(jnp.int32)
        table_v[last : last + 1, : offsets * blocks] = jnp.where(where < 0, total, where)


def kernel(shape, *refs):
    slots, block, offsets, nodes, feats = shape
    (
        rows, cols, table, features, cotangent, tiles, weight_one, weight_two,
        layer_out, feature_grad, one_out, two_out,
        tile, chain_f, chain_b, feat_flat, cot_flat, feat_v, cot_v, one, two,
        sib_1, za_1, zd_1, relay_1, sib_2, za_2, zd_2, relay_2,
        out_1, out_2, comb_1, comb_2, got_1, got_2, own_1, own_2,
        agg_send, spread_send, agg, spread, up_send, back_send, up, back,
        pre_v, act_v, grads, grad_sib, grad_chip, got_y, half, swapped, rounded, pieces, final, final_sib,
        local, sent, landed,
    ) = refs
    height, width = feat_flat.shape
    total_slots = offsets * slots
    blocks = width // block
    depth = agg.shape[0]
    share = agg.shape[1]
    PREV_F, PREV_B, LAST_F, LAST_B = range(4)
    none = total_slots

    me, mine = lax.axis_index("node"), lax.axis_index("feat")
    core = lax.rem(me, 2)
    sib = me + 1 - 2 * core
    ahead = lax.rem(me + 2 - 4 * core + nodes, nodes)
    behind = lax.rem(me - 2 + 4 * core + nodes, nodes)
    remote = Copies(sent, landed)

    loads = []
    for src, dst in (
        [(features, feat_flat), (cotangent, cot_flat)]
        + [
            (tiles.at[pl.ds(o * slots, slots)], tile.at[pl.ds(o * slots, slots)])
            for o in range(offsets)
        ]
        + [(weight_one, one), (weight_two, two)]
    ):
        copy = pltpu.make_async_copy(src, dst, local.at[len(loads)])
        copy.start()
        loads.append(copy)

    def by_blocks(flat, panel):
        def step(r, carry):
            panel[r] = flat[:, pl.ds(pl.multiple_of(r * block, block), block)]
            return carry

        lax.fori_loop(0, blocks, step, 0)

    barrier = pltpu.get_barrier_semaphore()
    half_nodes = nodes // 2

    def greet(node, feat):
        pl.semaphore_signal(barrier, inc=1, device_id=(node, feat), device_id_type=MESH)

    greet(sib, mine)
    for d in range(1, half_nodes):
        greet(lax.rem(me + 2 * d, nodes), mine)
    for d in range(1, feats):
        greet(me, lax.rem(mine + d, feats))
    loads[0].wait()
    by_blocks(feat_flat, feat_v)
    pl.semaphore_wait(barrier, half_nodes + feats - 1)

    def send_panel(panel, za, zd, sb):
        rows = blocks // CHUNKS
        parts = [
            remote.make(
                panel.at[pl.ds(k * rows, rows)], zd.at[pl.ds(k * rows, rows)], behind, mine
            )
            for k in range(CHUNKS)
        ]
        a = remote.make(panel, za, ahead, mine)
        s = remote.make(panel, sb, sib, mine)
        return parts, a, s

    def pass_on(parts, zd, relay):
        rows = blocks // CHUNKS
        relays = []
        for k, part in enumerate(parts):
            part.wait_recv()
            relays.append(
                remote.make(
                    zd.at[pl.ds(k * rows, rows)], relay.at[pl.ds(k * rows, rows)], sib, mine
                )
            )
        return relays

    def products(panel, o, take, prev, chain, contract):
        def step(g, carry):
            parts = []
            for i in range(GROUP):
                t = o * slots + g * GROUP + i
                parts.append(
                    lax.dot_general(
                        panel[take[t]],
                        tile[t],
                        contract,
                        preferred_element_type=F32,
                    )
                )
            for i in range(GROUP):
                t = o * slots + g * GROUP + i
                chain[t] = parts[i] + chain[table[prev, t]]
            return carry

        lax.fori_loop(0, slots // GROUP, step, 0)

    def forward(panel, o):
        products(panel, o, cols, PREV_F, chain_f, TAIL)

    def gather_forward(out):
        def step(r, carry):
            total = chain_f[table[LAST_F, r]]
            for o in range(1, offsets):
                total = total + chain_f[table[LAST_F, o * blocks + r]]
            out[:, pl.ds(pl.multiple_of(r * block, block), block)] = total.astype(out.dtype)
            return carry

        lax.fori_loop(0, blocks, step, 0)

    def backward(panel, o, out):
        products(panel, o, rows, PREV_B, chain_b, (((1,), (0,)), ((), ())))

        def step(r, carry):
            part = chain_b[table[LAST_B, o * blocks + r]]
            out[:, pl.ds(pl.multiple_of(r * block, block), block)] = part.astype(out.dtype)
            return carry

        lax.fori_loop(0, blocks, step, 0)

    def spread_early(panel, out, comb, got):
        p_dir, p_comb, p_add, p_sib = (out.at[k] for k in range(4))
        backward(panel, 1 + 2 * core, p_comb)
        c_comb = remote.make(p_comb, comb, sib, mine)
        backward(panel, 4 * core, p_dir)
        backward(panel, 4 - 4 * core, p_add)
        backward(panel, 3 - 2 * core, p_sib)
        return c_comb, remote.make(p_sib, got.at[2], sib, mine)

    def spread_late(before, c_comb, out, comb, got):
        parts, a = before
        p_dir, p_add = out.at[0], out.at[2]
        for part in parts:
            part.wait_send()
        c_dir = remote.make(p_dir, got.at[0], behind, mine)
        c_comb.wait_recv()
        p_add[...] = (p_add[...].astype(F32) + comb[...].astype(F32)).astype(BF16)
        a.wait_send()
        return c_dir, remote.make(p_add, got.at[1], ahead, mine)

    def collect(copies, got, own, out):
        for copy in copies:
            copy.wait_recv()
        total = own[...]
        for k in range(3):
            total = total + got[k].astype(F32)
        out[...] = total.astype(out.dtype)

    def rows_of(k):
        return pl.ds(pl.multiple_of(k * height, height), height)

    def columns_of(k):
        return pl.ds(pl.multiple_of(k * share, share), share)

    def to_rows(src, dst):
        copies = []
        for d in range(1, feats):
            peer = lax.rem(mine + d, feats)
            copies.append(
                remote.make(src.at[:, columns_of(peer)], dst.at[rows_of(mine)], me, peer)
            )
        dst[rows_of(mine)] = src[:, columns_of(mine)]
        return copies

    def to_features(src, dst):
        kept = share // block
        place = pl.ds(mine * kept, kept)
        copies = []
        for d in range(1, feats):
            peer = lax.rem(mine + d, feats)
            copies.append(remote.make(src.at[:, rows_of(peer)], dst.at[place], me, peer))
        dst[place] = src[:, rows_of(mine)]
        return copies

    def put_blocks(value, out):
        for k in range(share // block):
            out[k] = value[:, k * block : (k + 1) * block]

    def arrived(copies):
        for copy in copies:
            copy.wait_recv()

    parts, c_za, c_sb = send_panel(feat_v, za_1, zd_1, sib_1)
    chain_f[none] = jnp.zeros(chain_f.shape[1:], F32)
    chain_b[none] = jnp.zeros(chain_b.shape[1:], F32)
    loads[1].wait()
    by_blocks(cot_flat, cot_v)
    for copy in loads[2 : offsets + 2]:
        copy.wait()
    c_comb, c_own = spread_early(cot_v, out_1, comb_1, got_1)
    forward(feat_v, 2)
    c_sb.wait_recv()
    forward(sib_1, 3 - 2 * core)
    sums = (c_own, *spread_late((parts, c_za), c_comb, out_1, comb_1, got_1))
    relays = pass_on(parts, zd_1, relay_1)
    forward(zd_1, 4 - 4 * core)
    c_za.wait_recv()
    forward(za_1, 4 * core)
    arrived(relays)
    forward(relay_1, 1 + 2 * core)
    gather_forward(agg_send)
    agg_copies = to_rows(agg_send, agg)
    backward(cot_v, 2, own_1)
    collect(sums, got_1, own_1, spread_send)
    spread_copies = to_rows(spread_send, spread)

    dot = functools.partial(jnp.dot, preferred_element_type=F32)
    lead = (((0,), (0,)), ((), ()))
    loads[offsets + 2].wait()
    loads[offsets + 3].wait()
    arrived(agg_copies)
    pre = lax.dot_general(one[...], agg[...], lead, preferred_element_type=F32)
    pre_v[...] = pre
    act_v[...] = (pre * (1.0 / (1.0 + jnp.exp(-pre)))).astype(BF16)
    put_blocks(
        lax.dot_general(two[...], act_v[...], lead, preferred_element_type=F32).astype(BF16),
        up_send,
    )
    up_copies = to_features(up_send, up)
    arrived(spread_copies)
    act_back = dot(two[...], spread[...]).astype(BF16).astype(F32)
    pre = pre_v[...]
    sigma = 1.0 / (1.0 + jnp.exp(-pre))
    pre_back = (act_back * sigma * (1.0 + pre * (1.0 - sigma))).astype(BF16)
    put_blocks(dot(one[...], pre_back).astype(BF16), back_send)
    arrived(up_copies)
    parts, c_za, c_sb = send_panel(up, za_2, zd_2, sib_2)
    back_copies = to_features(back_send, back)
    grads[0] = lax.dot_general(agg[...], pre_back, TAIL, preferred_element_type=F32).astype(BF16)
    grads[1] = lax.dot_general(
        act_v[...], spread[...], TAIL, preferred_element_type=F32
    ).astype(BF16)
    c_grad = remote.make(grads.at[1 - core], grad_sib, sib, mine)

    forward(up, 2)
    c_grad.wait_recv()
    side = feats // SIDES * height
    added = grads[core].astype(F32) + grad_sib[...].astype(F32)
    for k in range(SIDES):
        grad_chip[k] = added[k * side : (k + 1) * side].astype(BF16)
    ring = feats // SIDES
    near, far = lax.rem(mine, ring), mine // ring
    ring_copies = []
    for d in range(1, ring):
        peer = lax.rem(near + d, ring)
        ring_copies.append(
            remote.make(grad_chip.at[:, rows_of(peer)], got_y.at[d - 1], me, far * ring + peer)
        )
    arrived(back_copies)
    p_dir, p_comb, p_add, p_sib = (out_2.at[k] for k in range(4))
    backward(back, 4 * core, p_dir)
    c_dir = remote.make(p_dir, got_2.at[0], behind, mine)
    arrived(ring_copies)
    total = grad_chip[:, rows_of(near)].astype(F32)
    for d in range(ring - 1):
        total = total + got_y[d].astype(F32)
    half[...] = total
    swap = remote.make(half.at[1 - far], swapped, me, (1 - far) * ring + near)
    backward(back, 1 + 2 * core, p_comb)
    c_comb = remote.make(p_comb, comb_2, sib, mine)
    backward(back, 4 - 4 * core, p_add)
    c_comb.wait_recv()
    p_add[...] = (p_add[...].astype(F32) + comb_2[...].astype(F32)).astype(BF16)
    c_add = remote.make(p_add, got_2.at[1], ahead, mine)

    groups = min(half_nodes, height // 16)
    splits = half_nodes // groups
    tall, wide = height // groups, depth // splits

    def piece(k):
        row, column = k // splits, lax.rem(k, splits)
        return (
            pl.ds(pl.multiple_of(row * tall, tall), tall),
            pl.ds(pl.multiple_of(column * wide, wide), wide),
        )

    place = me // 2
    others = [lax.rem(place + d, half_nodes) for d in range(1, half_nodes)]
    swap.wait_recv()
    added = swapped[...] + half[far]
    swapped[...] = added
    rounded[...] = added.astype(BF16)
    piece_copies = [
        remote.make(rounded.at[piece(peer)], pieces.at[d], 2 * peer + core, mine)
        for d, peer in enumerate(others)
    ]
    backward(back, 3 - 2 * core, p_sib)
    sums = c_dir, c_add, remote.make(p_sib, got_2.at[2], sib, mine)
    c_sb.wait_recv()
    forward(sib_2, 3 - 2 * core)
    relays = pass_on(parts, zd_2, relay_2)
    arrived(piece_copies)
    total = swapped[piece(place)]
    for d in range(half_nodes - 1):
        total = total + pieces[d].astype(F32)
    final[piece(place)] = total
    final_copies = [
        remote.make(final.at[piece(place)], final.at[piece(place)], 2 * peer + core, mine)
        for peer in others
    ]
    forward(zd_2, 4 - 4 * core)
    c_za.wait_recv()
    forward(za_2, 4 * core)
    arrived(relays)
    forward(relay_2, 1 + 2 * core)
    gather_forward(layer_out)
    arrived(final_copies)
    last = remote.make(final, final_sib, sib, mine)
    backward(back, 2, own_2)
    last.wait_recv()
    collect(sums, got_2, own_2, feature_grad)

    @pl.when(core == 0)
    def _():
        one_out[...] = final[...]
        two_out[...] = final_sib[...]

    @pl.when(core == 1)
    def _():
        one_out[...] = final_sib[...]
        two_out[...] = final[...]

    for copy in remote.all:
        copy.wait_send()


def give_kernel(*refs):
    half = len(refs) // 2
    for src, dst in zip(refs[:half], refs[half:]):
        dst[...] = src[...]


def on_device(features, tiles, tile_rows, tile_cols, counts, weight_one, weight_two, cotangent):
    offsets = counts.shape[0]
    slots = tile_rows.shape[0] // offsets
    block = tiles.shape[-1]
    height, width = features.shape
    depth = weight_one.shape[0]
    nodes, feats = lax.axis_size("node"), lax.axis_size("feat")
    share = width // feats
    lanes = -(-max(tile_rows.shape[0], offsets * (width // block)) // 128) * 128
    half_nodes = nodes // 2
    groups = min(half_nodes, height // 16)
    piece = (height // groups, depth * groups // half_nodes)
    remote_copies = (
        2 * (2 * CHUNKS + 6) + 4 * (feats - 1) + feats // SIDES - 1 + 3 + 2 * (half_nodes - 1)
    )
    flat = pltpu.VMEM((height, width), BF16)
    panel = pltpu.VMEM((width // block, height, block), BF16)
    stack = pltpu.VMEM((share // block, depth, block), BF16)
    chain = pltpu.VMEM((offsets * slots + 1, height, block), F32)
    square = pltpu.VMEM((depth, depth), BF16)
    side = pltpu.VMEM((depth, share), BF16)
    table = pl.pallas_call(
        functools.partial(table_kernel, slots, width // block),
        out_shape=jax.ShapeDtypeStruct((8, lanes), jnp.int32),
        in_specs=[SMEM, VMEM, VMEM],
        out_specs=VMEM,
    )(counts, tile_rows.reshape(1, -1), tile_cols.reshape(1, -1))
    made = pl.pallas_call(
        functools.partial(kernel, (slots, block, offsets, nodes, feats)),
        out_shape=[jax.ShapeDtypeStruct((height, width), BF16)] * 2
        + [jax.ShapeDtypeStruct((height, depth), F32)] * 2,
        in_specs=[SMEM] * 3 + [ANY] * 5,
        out_specs=[VMEM] * 4,
        scratch_shapes=[pltpu.VMEM(tiles.shape, BF16), chain, chain]
        + [flat, flat, panel, panel, square, square]
        + [panel] * 8
        + [pltpu.VMEM((4, height, width), BF16)] * 2
        + [flat] * 2
        + [pltpu.VMEM((3, height, width), BF16)] * 2
        + [pltpu.VMEM((height, width), F32)] * 2
        + [flat, flat, side, side, stack, stack, panel, panel]
        + [
            pltpu.VMEM((depth, share), F32),
            side,
            pltpu.VMEM((2, depth, depth), BF16),
            square,
            pltpu.VMEM((SIDES, depth // SIDES, depth), BF16),
            pltpu.VMEM((max(feats // SIDES - 1, 1), SIDES, height, depth), BF16),
            pltpu.VMEM((SIDES, height, depth), F32),
            pltpu.VMEM((height, depth), F32),
            pltpu.VMEM((height, depth), BF16),
            pltpu.VMEM((half_nodes - 1, *piece), BF16),
            pltpu.VMEM((height, depth), F32),
            pltpu.VMEM((height, depth), F32),
            pltpu.SemaphoreType.DMA((offsets + 4,)),
            pltpu.SemaphoreType.DMA((remote_copies,)),
            pltpu.SemaphoreType.DMA((remote_copies,)),
        ],
        compiler_params=pltpu.CompilerParams(
            collective_id=0, has_side_effects=True, vmem_limit_bytes=60 << 20
        ),
    )(
        tile_rows,
        tile_cols,
        table,
        features,
        cotangent,
        tiles,
        weight_one,
        weight_two,
    )
    return pl.pallas_call(
        give_kernel,
        out_shape=[jax.ShapeDtypeStruct(m.shape, m.dtype) for m in made],
        in_specs=[VMEM] * 4,
        out_specs=[VMEM] * 4,
    )(*made)


def solution(mesh):
    in_specs = (
        P("feat", "node"),
        P("node", None, None),
        P("node"),
        P("node"),
        P("node"),
        P(),
        P(),
        P("feat", "node"),
    )
    out_specs = (P("feat", "node"), P("feat", "node"), P("feat", None), P("feat", None))
    return jax.shard_map(
        on_device, mesh=mesh, in_specs=in_specs, out_specs=out_specs, check_vma=False
    )
```

```python
import functools

import jax
import jax.numpy as jnp
from jax import lax
from jax.experimental import pallas as pl
from jax.experimental.pallas import tpu as pltpu
from jax.sharding import PartitionSpec as P

GROUP = 8
CHUNKS = 2
SIDES = 2
MESH = pl.DeviceIdType.MESH
VMEM = pl.BlockSpec(memory_space=pltpu.VMEM)
SMEM = pl.BlockSpec(memory_space=pltpu.SMEM)
ANY = pl.BlockSpec(memory_space=pl.ANY)
TAIL = (((1,), (1,)), ((), ()))
BF16, F32 = jnp.bfloat16, jnp.float32


class Copy:
    def __init__(self, copy):
        self.copy, self.left = copy, False
        copy.start()

    def wait_recv(self):
        self.copy.wait_recv()

    def wait_send(self):
        if not self.left:
            self.copy.wait_send()
        self.left = True


class Copies:
    def __init__(self, sent, landed):
        self.sent, self.landed, self.all = sent, landed, []

    def make(self, src, dst, node, feat):
        k = len(self.all)
        copy = Copy(
            pltpu.make_async_remote_copy(
                src_ref=src,
                dst_ref=dst,
                send_sem=self.sent.at[k],
                recv_sem=self.landed.at[k],
                device_id=(node, feat),
                device_id_type=MESH,
            )
        )
        self.all.append(copy)
        return copy


def table_kernel(slots, blocks, counts, rows_v, cols_v, table_v):
    offsets, total = counts.shape[0], rows_v.shape[1]
    iota = functools.partial(lax.broadcasted_iota, jnp.int32)
    down, along = iota((total, total), 0), iota((total, total), 1)

    def place(index, size, count):
        group = jnp.zeros_like(index)
        for k in range(1, count):
            group = group + (index >= k * size).astype(jnp.int32)
        return group

    close = (down < along) & (place(down, slots, offsets) == place(along, slots, offsets))
    line = iota((total, 1), 0)
    owner = place(line, slots, offsets)
    limit = jnp.zeros_like(line)
    for o in range(offsets):
        limit = jnp.where(owner == o, o * slots + counts[o], limit)
    spots = iota((1, offsets * blocks), 1)
    group = place(spots, blocks, offsets)
    for keys_v, prev, last in ((rows_v, 0, 2), (cols_v, 1, 3)):
        keys = keys_v[...].astype(F32)
        column = jnp.sum(jnp.where(down == along, keys, 0.0), axis=1, keepdims=True)
        where = jnp.max(
            jnp.where(close & (column == keys), down.astype(F32), -1.0), axis=0, keepdims=True
        ).astype(jnp.int32)
        table_v[prev : prev + 1, :total] = jnp.where(where < 0, total, where)
        wanted = (spots - group * blocks).astype(F32)
        mine = (column == wanted) & (owner == group) & (line < limit)
        where = jnp.max(
            jnp.where(mine, line.astype(F32), -1.0), axis=0, keepdims=True
        ).astype(jnp.int32)
        table_v[last : last + 1, : offsets * blocks] = jnp.where(where < 0, total, where)


def kernel(shape, *refs):
    slots, block, offsets, nodes, feats = shape
    (
        rows, cols, table, features, cotangent, tiles, weight_one, weight_two,
        layer_out, feature_grad, one_out, two_out,
        tile, chain_f, chain_b, feat_flat, cot_flat, feat_v, cot_v, one, two,
        sib_1, za_1, zd_1, relay_1, sib_2, za_2, zd_2, relay_2,
        out_1, out_2, comb_1, comb_2, got_1, got_2, own_1, own_2,
        agg_send, spread_send, agg, spread, up_send, back_send, up, back,
        pre_v, act_v, grads, grad_sib, grad_chip, got_y, half, swapped, rounded, pieces, final, final_sib,
        local, sent, landed,
    ) = refs
    height, width = feat_flat.shape
    total_slots = offsets * slots
    blocks = width // block
    depth = agg.shape[0]
    share = agg.shape[1]
    PREV_F, PREV_B, LAST_F, LAST_B = range(4)
    none = total_slots

    me, mine = lax.axis_index("node"), lax.axis_index("feat")
    core = lax.rem(me, 2)
    sib = me + 1 - 2 * core
    ahead = lax.rem(me + 2 - 4 * core + nodes, nodes)
    behind = lax.rem(me - 2 + 4 * core + nodes, nodes)
    remote = Copies(sent, landed)

    loads = []
    for src, dst in (
        [(features, feat_flat), (cotangent, cot_flat)]
        + [
            (tiles.at[pl.ds(o * slots, slots)], tile.at[pl.ds(o * slots, slots)])
            for o in range(offsets)
        ]
        + [(weight_one, one), (weight_two, two)]
    ):
        copy = pltpu.make_async_copy(src, dst, local.at[len(loads)])
        copy.start()
        loads.append(copy)

    def by_blocks(flat, panel):
        def step(r, carry):
            panel[r] = flat[:, pl.ds(pl.multiple_of(r * block, block), block)]
            return carry

        lax.fori_loop(0, blocks, step, 0)

    barrier = pltpu.get_barrier_semaphore()
    half_nodes = nodes // 2

    def greet(node, feat):
        pl.semaphore_signal(barrier, inc=1, device_id=(node, feat), device_id_type=MESH)

    greet(sib, mine)
    for d in range(1, half_nodes):
        greet(lax.rem(me + 2 * d, nodes), mine)
    for d in range(1, feats):
        greet(me, lax.rem(mine + d, feats))
    loads[0].wait()
    by_blocks(feat_flat, feat_v)
    pl.semaphore_wait(barrier, half_nodes + feats - 1)

    def send_panel(panel, za, zd, sb):
        rows = blocks // CHUNKS
        parts = [
            remote.make(
                panel.at[pl.ds(k * rows, rows)], zd.at[pl.ds(k * rows, rows)], behind, mine
            )
            for k in range(CHUNKS)
        ]
        a = remote.make(panel, za, ahead, mine)
        s = remote.make(panel, sb, sib, mine)
        return parts, a, s

    def pass_on(parts, zd, relay):
        rows = blocks // CHUNKS
        relays = []
        for k, part in enumerate(parts):
            part.wait_recv()
            relays.append(
                remote.make(
                    zd.at[pl.ds(k * rows, rows)], relay.at[pl.ds(k * rows, rows)], sib, mine
                )
            )
        return relays

    def products(panel, o, take, prev, chain, contract):
        def step(g, carry):
            parts = []
            for i in range(GROUP):
                t = o * slots + g * GROUP + i
                parts.append(
                    lax.dot_general(
                        panel[take[t]],
                        tile[t],
                        contract,
                        preferred_element_type=F32,
                    )
                )
            for i in range(GROUP):
                t = o * slots + g * GROUP + i
                chain[t] = parts[i] + chain[table[prev, t]]
            return carry

        lax.fori_loop(0, slots // GROUP, step, 0)

    def forward(panel, o):
        products(panel, o, cols, PREV_F, chain_f, TAIL)

    def gather_forward(out):
        def step(r, carry):
            total = chain_f[table[LAST_F, r]]
            for o in range(1, offsets):
                total = total + chain_f[table[LAST_F, o * blocks + r]]
            out[:, pl.ds(pl.multiple_of(r * block, block), block)] = total.astype(out.dtype)
            return carry

        lax.fori_loop(0, blocks, step, 0)

    def backward(panel, o, out):
        products(panel, o, rows, PREV_B, chain_b, (((1,), (0,)), ((), ())))

        def step(r, carry):
            part = chain_b[table[LAST_B, o * blocks + r]]
            out[:, pl.ds(pl.multiple_of(r * block, block), block)] = part.astype(out.dtype)
            return carry

        lax.fori_loop(0, blocks, step, 0)

    def spread_early(panel, out, comb, got):
        p_dir, p_comb, p_add, p_sib = (out.at[k] for k in range(4))
        backward(panel, 1 + 2 * core, p_comb)
        c_comb = remote.make(p_comb, comb, sib, mine)
        backward(panel, 4 * core, p_dir)
        backward(panel, 4 - 4 * core, p_add)
        backward(panel, 3 - 2 * core, p_sib)
        return c_comb, remote.make(p_sib, got.at[2], sib, mine)

    def spread_late(before, c_comb, out, comb, got):
        parts, a = before
        p_dir, p_add = out.at[0], out.at[2]
        for part in parts:
            part.wait_send()
        c_dir = remote.make(p_dir, got.at[0], behind, mine)
        c_comb.wait_recv()
        p_add[...] = (p_add[...].astype(F32) + comb[...].astype(F32)).astype(BF16)
        a.wait_send()
        return c_dir, remote.make(p_add, got.at[1], ahead, mine)

    def collect(copies, got, own, out):
        for copy in copies:
            copy.wait_recv()
        total = own[...]
        for k in range(3):
            total = total + got[k].astype(F32)
        out[...] = total.astype(out.dtype)

    def rows_of(k):
        return pl.ds(pl.multiple_of(k * height, height), height)

    def columns_of(k):
        return pl.ds(pl.multiple_of(k * share, share), share)

    def to_rows(src, dst):
        copies = []
        for d in range(1, feats):
            peer = lax.rem(mine + d, feats)
            copies.append(
                remote.make(src.at[:, columns_of(peer)], dst.at[rows_of(mine)], me, peer)
            )
        dst[rows_of(mine)] = src[:, columns_of(mine)]
        return copies

    def to_features(src, dst):
        kept = share // block
        place = pl.ds(mine * kept, kept)
        copies = []
        for d in range(1, feats):
            peer = lax.rem(mine + d, feats)
            copies.append(remote.make(src.at[:, rows_of(peer)], dst.at[place], me, peer))
        dst[place] = src[:, rows_of(mine)]
        return copies

    def put_blocks(value, out):
        for k in range(share // block):
            out[k] = value[:, k * block : (k + 1) * block]

    def arrived(copies):
        for copy in copies:
            copy.wait_recv()

    parts, c_za, c_sb = send_panel(feat_v, za_1, zd_1, sib_1)
    chain_f[none] = jnp.zeros(chain_f.shape[1:], F32)
    chain_b[none] = jnp.zeros(chain_b.shape[1:], F32)
    loads[1].wait()
    by_blocks(cot_flat, cot_v)
    for copy in loads[2 : offsets + 2]:
        copy.wait()
    c_comb, c_own = spread_early(cot_v, out_1, comb_1, got_1)
    forward(feat_v, 2)
    c_sb.wait_recv()
    forward(sib_1, 3 - 2 * core)
    sums = (c_own, *spread_late((parts, c_za), c_comb, out_1, comb_1, got_1))
    relays = pass_on(parts, zd_1, relay_1)
    forward(zd_1, 4 - 4 * core)
    c_za.wait_recv()
    forward(za_1, 4 * core)
    arrived(relays)
    forward(relay_1, 1 + 2 * core)
    gather_forward(agg_send)
    agg_copies = to_rows(agg_send, agg)
    backward(cot_v, 2, own_1)
    collect(sums, got_1, own_1, spread_send)
    spread_copies = to_rows(spread_send, spread)

    dot = functools.partial(jnp.dot, preferred_element_type=F32)
    lead = (((0,), (0,)), ((), ()))
    loads[offsets + 2].wait()
    loads[offsets + 3].wait()
    arrived(agg_copies)
    pre = lax.dot_general(one[...], agg[...], lead, preferred_element_type=F32)
    pre_v[...] = pre
    act_v[...] = (pre * (1.0 / (1.0 + jnp.exp(-pre)))).astype(BF16)
    put_blocks(
        lax.dot_general(two[...], act_v[...], lead, preferred_element_type=F32).astype(BF16),
        up_send,
    )
    up_copies = to_features(up_send, up)
    arrived(spread_copies)
    act_back = dot(two[...], spread[...]).astype(BF16).astype(F32)
    pre = pre_v[...]
    sigma = 1.0 / (1.0 + jnp.exp(-pre))
    pre_back = (act_back * sigma * (1.0 + pre * (1.0 - sigma))).astype(BF16)
    put_blocks(dot(one[...], pre_back).astype(BF16), back_send)
    back_copies = to_features(back_send, back)
    grads[0] = lax.dot_general(agg[...], pre_back, TAIL, preferred_element_type=F32).astype(BF16)
    grads[1] = lax.dot_general(
        act_v[...], spread[...], TAIL, preferred_element_type=F32
    ).astype(BF16)
    c_grad = remote.make(grads.at[1 - core], grad_sib, sib, mine)

    arrived(up_copies)
    for copy in back_copies:
        copy.wait_send()
    parts, c_za, c_sb = send_panel(up, za_2, zd_2, sib_2)

    c_grad.wait_recv()
    side = feats // SIDES * height
    added = grads[core].astype(F32) + grad_sib[...].astype(F32)
    for k in range(SIDES):
        grad_chip[k] = added[k * side : (k + 1) * side].astype(BF16)
    ring = feats // SIDES
    near, far = lax.rem(mine, ring), mine // ring
    ring_copies = []
    for d in range(1, ring):
        peer = lax.rem(near + d, ring)
        ring_copies.append(
            remote.make(grad_chip.at[:, rows_of(peer)], got_y.at[d - 1], me, far * ring + peer)
        )
    forward(up, 2)
    c_sb.wait_recv()
    forward(sib_2, 3 - 2 * core)
    arrived(ring_copies)
    total = grad_chip[:, rows_of(near)].astype(F32)
    for d in range(ring - 1):
        total = total + got_y[d].astype(F32)
    half[...] = total
    swap = remote.make(half.at[1 - far], swapped, me, (1 - far) * ring + near)
    arrived(back_copies)
    p_dir, p_comb, p_add, p_sib = (out_2.at[k] for k in range(4))
    backward(back, 4 * core, p_dir)
    c_dir = remote.make(p_dir, got_2.at[0], behind, mine)
    groups = min(half_nodes, height // 16)
    splits = half_nodes // groups
    tall, wide = height // groups, depth // splits

    def piece(k):
        row, column = k // splits, lax.rem(k, splits)
        return (
            pl.ds(pl.multiple_of(row * tall, tall), tall),
            pl.ds(pl.multiple_of(column * wide, wide), wide),
        )

    place = me // 2
    others = [lax.rem(place + d, half_nodes) for d in range(1, half_nodes)]
    swap.wait_recv()
    added = swapped[...] + half[far]
    swapped[...] = added
    rounded[...] = added.astype(BF16)
    piece_copies = [
        remote.make(rounded.at[piece(peer)], pieces.at[d], 2 * peer + core, mine)
        for d, peer in enumerate(others)
    ]
    backward(back, 1 + 2 * core, p_comb)
    c_comb = remote.make(p_comb, comb_2, sib, mine)
    backward(back, 4 - 4 * core, p_add)
    c_comb.wait_recv()
    p_add[...] = (p_add[...].astype(F32) + comb_2[...].astype(F32)).astype(BF16)
    c_add = remote.make(p_add, got_2.at[1], ahead, mine)

    arrived(piece_copies)
    total = swapped[piece(place)]
    for d in range(half_nodes - 1):
        total = total + pieces[d].astype(F32)
    final[piece(place)] = total
    final_copies = [
        remote.make(final.at[piece(place)], final.at[piece(place)], 2 * peer + core, mine)
        for peer in others
    ]
    backward(back, 3 - 2 * core, p_sib)
    sums = c_dir, c_add, remote.make(p_sib, got_2.at[2], sib, mine)
    relays = pass_on(parts, zd_2, relay_2)
    forward(zd_2, 4 - 4 * core)
    c_za.wait_recv()
    forward(za_2, 4 * core)
    arrived(relays)
    forward(relay_2, 1 + 2 * core)
    gather_forward(layer_out)
    arrived(final_copies)
    last = remote.make(final, final_sib, sib, mine)
    backward(back, 2, own_2)
    last.wait_recv()
    collect(sums, got_2, own_2, feature_grad)

    @pl.when(core == 0)
    def _():
        one_out[...] = final[...]
        two_out[...] = final_sib[...]

    @pl.when(core == 1)
    def _():
        one_out[...] = final_sib[...]
        two_out[...] = final[...]

    for copy in remote.all:
        copy.wait_send()


def give_kernel(*refs):
    half = len(refs) // 2
    for src, dst in zip(refs[:half], refs[half:]):
        dst[...] = src[...]


def on_device(features, tiles, tile_rows, tile_cols, counts, weight_one, weight_two, cotangent):
    offsets = counts.shape[0]
    slots = tile_rows.shape[0] // offsets
    block = tiles.shape[-1]
    height, width = features.shape
    depth = weight_one.shape[0]
    nodes, feats = lax.axis_size("node"), lax.axis_size("feat")
    share = width // feats
    lanes = -(-max(tile_rows.shape[0], offsets * (width // block)) // 128) * 128
    half_nodes = nodes // 2
    groups = min(half_nodes, height // 16)
    piece = (height // groups, depth * groups // half_nodes)
    remote_copies = (
        2 * (2 * CHUNKS + 6) + 4 * (feats - 1) + feats // SIDES - 1 + 3 + 2 * (half_nodes - 1)
    )
    flat = pltpu.VMEM((height, width), BF16)
    panel = pltpu.VMEM((width // block, height, block), BF16)
    stack = pltpu.VMEM((share // block, depth, block), BF16)
    chain = pltpu.VMEM((offsets * slots + 1, height, block), F32)
    square = pltpu.VMEM((depth, depth), BF16)
    side = pltpu.VMEM((depth, share), BF16)
    table = pl.pallas_call(
        functools.partial(table_kernel, slots, width // block),
        out_shape=jax.ShapeDtypeStruct((8, lanes), jnp.int32),
        in_specs=[SMEM, VMEM, VMEM],
        out_specs=VMEM,
    )(counts, tile_rows.reshape(1, -1), tile_cols.reshape(1, -1))
    made = pl.pallas_call(
        functools.partial(kernel, (slots, block, offsets, nodes, feats)),
        out_shape=[jax.ShapeDtypeStruct((height, width), BF16)] * 2
        + [jax.ShapeDtypeStruct((height, depth), F32)] * 2,
        in_specs=[SMEM] * 3 + [ANY] * 5,
        out_specs=[VMEM] * 4,
        scratch_shapes=[pltpu.VMEM(tiles.shape, BF16), chain, chain]
        + [flat, flat, panel, panel, square, square]
        + [panel] * 8
        + [pltpu.VMEM((4, height, width), BF16)] * 2
        + [flat] * 2
        + [pltpu.VMEM((3, height, width), BF16)] * 2
        + [pltpu.VMEM((height, width), F32)] * 2
        + [flat, flat, side, side, stack, stack, panel, panel]
        + [
            pltpu.VMEM((depth, share), F32),
            side,
            pltpu.VMEM((2, depth, depth), BF16),
            square,
            pltpu.VMEM((SIDES, depth // SIDES, depth), BF16),
            pltpu.VMEM((max(feats // SIDES - 1, 1), SIDES, height, depth), BF16),
            pltpu.VMEM((SIDES, height, depth), F32),
            pltpu.VMEM((height, depth), F32),
            pltpu.VMEM((height, depth), BF16),
            pltpu.VMEM((half_nodes - 1, *piece), BF16),
            pltpu.VMEM((height, depth), F32),
            pltpu.VMEM((height, depth), F32),
            pltpu.SemaphoreType.DMA((offsets + 4,)),
            pltpu.SemaphoreType.DMA((remote_copies,)),
            pltpu.SemaphoreType.DMA((remote_copies,)),
        ],
        compiler_params=pltpu.CompilerParams(
            collective_id=0, has_side_effects=True, vmem_limit_bytes=60 << 20
        ),
    )(
        tile_rows,
        tile_cols,
        table,
        features,
        cotangent,
        tiles,
        weight_one,
        weight_two,
    )
    return pl.pallas_call(
        give_kernel,
        out_shape=[jax.ShapeDtypeStruct(m.shape, m.dtype) for m in made],
        in_specs=[VMEM] * 4,
        out_specs=[VMEM] * 4,
    )(*made)


def solution(mesh):
    in_specs = (
        P("feat", "node"),
        P("node", None, None),
        P("node"),
        P("node"),
        P("node"),
        P(),
        P(),
        P("feat", "node"),
    )
    out_specs = (P("feat", "node"), P("feat", "node"), P("feat", None), P("feat", None))
    return jax.shard_map(
        on_device, mesh=mesh, in_specs=in_specs, out_specs=out_specs, check_vma=False
    )
```
